32 devices in a mesh: pb: 4 (over y, core), kv: 8 (over z, x).
Axes of the slice: x: 2, y: 2, z: 4, core: 2. Of those that a mesh axis runs over, the one named last changes fastest.
Arguments:
- queries: bfloat16 [8192, 128], P(('pb', 'kv')), may hold values from -15 to 15
- query_tangent: bfloat16 [8192, 128], P(('pb', 'kv')), may hold values from -2 to 2
- keys: bfloat16 [8192, 128], P(('pb', 'kv')), may hold values from -8 to 8
- values: bfloat16 [8192, 128], P(('pb', 'kv')), may hold values from -6 to 6
- key_tangent: bfloat16 [8192, 128], P(('pb', 'kv')), may hold values from -2 to 2
- value_tangent: bfloat16 [8192, 128], P(('pb', 'kv')), may hold values from -6 to 6
- block_list: int32 [64, 8, 8], P('pb', 'kv'), may hold values from 0 to 63, as said below
- block_count: int32 [64, 8], P('pb', 'kv'), may hold values from 1 to 8, as said below
Outputs:
- attended: bfloat16 [8192, 128], P(('pb', 'kv'))
- attended_tangent: bfloat16 [8192, 128], P(('pb', 'kv'))
The draws below stay inside these ranges and needn't reach their ends.
Inputs may be any that keep to these rules, and one draw needn't show every extreme that they name: `block_list`: entries for one query block and slab j are distinct key blocks g whose index g // (256 // 128) leaves remainder j when divided by 8; entries past block_count are valid but unused. `block_count`: the value 8 is reached in every key slab.
All inputs are finite; a program needn't handle non-finite values.
Results may differ from the reference program's by a relative error of at most 0.01.
Values may be sent and summed in bfloat16 or wider, within the bound.
A program may use at most 128 MiB of HBM per device.

```python
import math
import jax
import jax.numpy as jnp
from jax import lax

HD = 128
BLK = 128
LMAX = 8
TOK_DEV = 256
SEQ = 8192
QBLOCKS = 64
KSLABS = 8


def draw_queries(key, part):
    result = jnp.clip(2.5 * jax.random.normal(key, (SEQ, HD), jnp.float32), -15.0, 15.0)
    return result.astype(jnp.bfloat16)


def draw_keys(key, part):
    noise = jax.random.normal(jax.random.fold_in(key, 3), (SEQ, HD), jnp.float32)
    result = jnp.clip(noise, -6.0, 6.0)
    return result.astype(jnp.bfloat16)


def block_tables(key):
    base = jax.random.fold_in(key, 7)
    level_key, raw_key, force_key, order_key = jax.random.split(base, 4)
    slab_blocks = SEQ // (BLK * KSLABS)
    shard_blocks = TOK_DEV // BLK
    per_query_slab = QBLOCKS // (SEQ // (TOK_DEV * KSLABS))
    level = jax.random.randint(level_key, (SEQ // (TOK_DEV * KSLABS), KSLABS), 1, LMAX + 1)
    row_level = jnp.repeat(level, per_query_slab, axis=0)
    raw = jax.random.randint(raw_key, (QBLOCKS, KSLABS), 0, 1 << 20)
    counts = 1 + raw % row_level
    forced = jax.random.randint(force_key, (KSLABS,), 0, QBLOCKS)
    counts = jnp.where(jnp.arange(QBLOCKS)[:, None] == forced[None, :], LMAX, counts)
    ranks = jax.random.randint(order_key, (QBLOCKS, KSLABS, slab_blocks), 0, 1 << 20)
    ranks = ranks * slab_blocks + jnp.arange(slab_blocks)[None, None, :]
    picked = jnp.argsort(ranks, axis=-1, stable=True)[:, :, :LMAX]
    slab_index = jnp.arange(KSLABS)[None, :, None]
    global_block = (picked // shard_blocks * KSLABS + slab_index) * shard_blocks + picked % shard_blocks
    return (global_block.astype(jnp.int32), counts.astype(jnp.int32))


def draw_block_list(key, part):
    return block_tables(key)[0]


def draw_block_count(key, part):
    return block_tables(key)[1]


def steps_of(stream_key, dims, pieces, least, largest):
    def one(axis_at, parts):
        steps = jax.random.uniform(jax.random.fold_in(jax.random.fold_in(stream_key, 6), axis_at), (parts,), jnp.float32, least / len(pieces), largest / len(pieces))
        return jnp.repeat(jnp.exp(steps), dims[axis_at] // parts).reshape((-1,) + (1,) * (len(dims) - axis_at - 1))

    gain = one(*pieces[0])
    for cut in pieces[1:]:
        gain = gain * one(*cut)
    return gain


def bell_draw(stream_key, dims, deviation, limit, pieces=(), kind=jnp.bfloat16):
    values = jax.random.normal(stream_key, dims, jnp.float32) * deviation
    if len(pieces) > 0:
        values = steps_of(stream_key, dims, pieces, -0.22, 0.18) * values
    return jnp.clip(values, min=-limit, max=limit).astype(kind)


def setup_inputs(seed: int = 0) -> dict:
    streams_of = jax.random.split(jax.random.key(seed), 9)
    return {
        "queries": draw_queries(jax.random.fold_in(streams_of[8], 71), 0),
        "query_tangent": bell_draw(streams_of[1], (SEQ, HD), 0.3, 2.0, ((0, 32),)),
        "keys": draw_keys(jax.random.fold_in(streams_of[8], 71), 0),
        "values": bell_draw(streams_of[3], (SEQ, HD), 1.0, 6.0, ((0, 32),)),
        "key_tangent": bell_draw(streams_of[4], (SEQ, HD), 0.3, 2.0, ((0, 32),)),
        "value_tangent": bell_draw(streams_of[5], (SEQ, HD), 1.0, 6.0, ((0, 32),)),
        "block_list": draw_block_list(jax.random.fold_in(streams_of[8], 71), 0),
        "block_count": draw_block_count(jax.random.fold_in(streams_of[8], 71), 0),
    }


def reference(queries, query_tangent, keys, values, key_tangent, value_tangent, block_list, block_count):
    score_scale = 1.0 / math.sqrt(HD)
    key_blocks = keys.reshape(QBLOCKS, BLK, HD)
    value_blocks = values.reshape(QBLOCKS, BLK, HD)
    keyt_blocks = key_tangent.reshape(QBLOCKS, BLK, HD)
    valuet_blocks = value_tangent.reshape(QBLOCKS, BLK, HD)

    def one_block(items):
        query_block, tangent_block, picked, counts = items
        flat = picked.reshape(-1)
        key_rows = key_blocks[flat].reshape(-1, HD)
        value_rows = value_blocks[flat].reshape(-1, HD)
        keyt_rows = keyt_blocks[flat].reshape(-1, HD)
        valuet_rows = valuet_blocks[flat].reshape(-1, HD)
        active = jnp.repeat((jnp.arange(LMAX)[None, :] < counts[:, None]).reshape(-1), BLK)
        scores = jnp.dot(query_block, key_rows.T, preferred_element_type=jnp.float32) * score_scale
        score_tangent = (jnp.dot(tangent_block, key_rows.T, preferred_element_type=jnp.float32) + jnp.dot(query_block, keyt_rows.T, preferred_element_type=jnp.float32)) * score_scale
        peak = lax.optimization_barrier(jnp.max(jnp.where(active[None, :], scores, -jnp.inf), axis=1))
        weights = jnp.where(active[None, :], jnp.exp(scores - peak[:, None]), 0.0)
        total = lax.optimization_barrier(jnp.sum(weights, axis=1))
        slope = lax.optimization_barrier(jnp.sum(weights * score_tangent, axis=1))
        weights_b = weights.astype(jnp.bfloat16)
        scaled_b = (weights * score_tangent).astype(jnp.bfloat16)
        weighted = jnp.dot(weights_b, value_rows, preferred_element_type=jnp.float32)
        tangent_sum = jnp.dot(scaled_b, value_rows, preferred_element_type=jnp.float32) + jnp.dot(weights_b, valuet_rows, preferred_element_type=jnp.float32)
        output = weighted / total[:, None]
        output_tangent = tangent_sum / total[:, None] - (slope / total)[:, None] * output
        return (output.astype(jnp.bfloat16), output_tangent.astype(jnp.bfloat16))
    query_blocks = queries.reshape(QBLOCKS, BLK, HD)
    tangent_blocks = query_tangent.reshape(QBLOCKS, BLK, HD)
    attended, attended_tangent = lax.map(one_block, (query_blocks, tangent_blocks, block_list, block_count))
    return (attended.reshape(SEQ, HD), attended_tangent.reshape(SEQ, HD))
```

```python
import functools
import math

import jax
import jax.numpy as jnp
from jax import lax
from jax.experimental import pallas as pl
from jax.experimental.pallas import tpu as pltpu
from jax.sharding import PartitionSpec as P

BLK = 128
NT = (((1,), (1,)), ((), ()))
MESH = pl.DeviceIdType.MESH


def flip(a, b, bits):
    out = 0
    for k in range(bits):
        w = 1 << k
        out = out + (a // w + b // w) % 2 * w
    return out


def kernel(
    zc, q_in, qt_in, k_in, v_in, kt_in, vt_in, bias_in, out_ref, outt_ref,
    kv, qq, bias_x, s_scr, p_scr, ps_scr, send, sstat, recv, rstat, coef,
    local_sem, ks, kr, qs, qr, bs, rs, rr, ts, tr,
):
    rows, hd = q_in.shape
    half = rows // 2
    bits = zc.bit_length() - 1
    scale = 1.0 / math.sqrt(hd)
    factor = scale * math.log2(math.e)
    pb, kvi = lax.axis_index("pb"), lax.axis_index("kv")
    y, c, z, x = pb // 2, pb % 2, kvi // 2, kvi % 2
    to_x = (pb, kvi + 1 - 2 * x)
    to_y = (pb + 2 - 4 * y, kvi)
    to_c = (pb + 1 - 2 * c, kvi)

    def to_z(mask):
        return (pb, flip(z, mask, bits) * 2 + x)

    loads = []
    for n, (src, dst) in enumerate(
        [
            (k_in, kv.at[0, :, pl.ds(0, hd)]),
            (kt_in, kv.at[0, :, pl.ds(hd, hd)]),
            (v_in, kv.at[0, :, pl.ds(2 * hd, hd)]),
            (vt_in, kv.at[0, :, pl.ds(3 * hd, hd)]),
            (qt_in, qq.at[0, :, pl.ds(0, hd)]),
            (q_in, qq.at[0, :, pl.ds(hd, hd)]),
        ]
    ):
        copy = pltpu.make_async_copy(src, dst, local_sem.at[n])
        copy.start()
        loads.append(copy)

    barrier = pltpu.get_barrier_semaphore()
    for dev in [to_x, to_y, to_c] + [to_z(m) for m in range(1, zc)]:
        pl.semaphore_signal(barrier, inc=1, device_id=dev, device_id_type=MESH)
    pl.semaphore_wait(barrier, 2 + zc)
    for copy in loads:
        copy.wait()

    def remote(src, dst, ssem, rsem, dev):
        return pltpu.make_async_remote_copy(
            src_ref=src, dst_ref=dst, send_sem=ssem, recv_sem=rsem,
            device_id=dev, device_id_type=MESH,
        )

    sent = []

    def piece(slot, h):
        return kv.at[slot, pl.ds(h * half, half)]

    def give(slot, h, dst, dev):
        copy = remote(piece(slot, h), piece(dst, h), ks.at[dst, h], kr.at[dst, h], dev)
        copy.start()
        sent.append(copy)

    def got(slot, h):
        remote(piece(slot, h), piece(slot, h), ks.at[slot, h], kr.at[slot, h], to_c).wait_recv()

    give(0, 1, 1, to_x)
    give(0, 0, 2, to_y)
    give(0, 0, 1, to_x)
    give(0, 1, 2, to_y)
    for m in range(zc - 1, 0, -1):
        copy = remote(qq.at[0], qq.at[m], qs.at[m], qr.at[m], to_z(m))
        copy.start()
        sent.append(copy)
    give(0, 0, 4, to_c)
    give(0, 1, 4, to_c)
    bias_copy = remote(bias_in.at[1 - x], bias_x, bs.at[0], bs.at[1], to_x)
    bias_copy.start()
    got(2, 0)
    give(2, 0, 3, to_x)
    give(2, 0, 6, to_c)
    got(1, 1)
    give(1, 1, 3, to_y)
    give(1, 1, 5, to_c)
    got(1, 0)
    give(1, 0, 5, to_c)
    got(2, 1)
    give(2, 1, 6, to_c)
    got(3, 0)
    give(3, 0, 7, to_c)
    got(3, 1)
    give(3, 1, 7, to_c)
    bias_copy.wait_recv()
    for slot in range(4, 8):
        for h in range(2):
            got(slot, h)

    def attend(mask):
        zt = flip(z, mask, bits)
        best = None
        for r in range(8):
            pbr = flip(pb, (r // 2) % 2 * 2 + r // 4, 2)
            if r % 2 == 0:
                b = bias_in[x, pbr, zt]
            else:
                b = bias_x[pbr, zt]
            s = lax.dot_general(
                qq[mask, :, hd:], kv[r, :, 0:hd], NT, preferred_element_type=jnp.float32
            )
            s = (s.reshape(2, half, rows) + b[:, None, :]).reshape(rows, rows)
            s_scr[:, r * rows : (r + 1) * rows] = s
            top = jnp.maximum(s[:, :hd], s[:, hd:])
            best = top if best is None else jnp.maximum(best, top)
        peak = jnp.max(best, axis=1, keepdims=True)
        total = slope = None
        for r in range(8):
            p = jnp.exp2((s_scr[:, r * rows : (r + 1) * rows] - peak) * factor)
            t = lax.dot_general(
                qq[mask], kv[r, :, 0 : 2 * hd], NT, preferred_element_type=jnp.float32
            )
            pt = p * t
            p_scr[:, r * rows : (r + 1) * rows] = p.astype(jnp.bfloat16)
            ps_scr[:, r * rows : (r + 1) * rows] = pt.astype(jnp.bfloat16)
            p2 = p[:, :hd] + p[:, hd:]
            pt2 = pt[:, :hd] + pt[:, hd:]
            total = p2 if total is None else total + p2
            slope = pt2 if slope is None else slope + pt2
        total = jnp.sum(total, axis=1, keepdims=True)
        slope = jnp.sum(slope, axis=1, keepdims=True) * scale
        both = jnp.dot(
            p_scr[...], kv[:, :, 2 * hd :].reshape(8 * rows, 2 * hd),
            preferred_element_type=jnp.float32,
        )
        tang = jnp.dot(
            ps_scr[...], kv[:, :, 2 * hd : 3 * hd].reshape(8 * rows, hd),
            preferred_element_type=jnp.float32,
        )
        weighted = both[:, :hd]
        mean = slope / total
        centred = tang * scale + both[:, hd:] - mean * weighted
        lane = lax.broadcasted_iota(jnp.int32, (rows, hd), 1)
        stats = jnp.where(lane == 0, peak, jnp.where(lane == 1, total, mean))
        return weighted, centred, stats.T[0:8]

    def result_copies(mask):
        dev = to_z(mask)
        return (
            remote(send.at[mask], recv.at[mask], rs.at[mask], rr.at[mask], dev),
            remote(sstat.at[mask], rstat.at[mask], ts.at[mask], tr.at[mask], dev),
        )

    def step(t, carry):
        mask = zc - 1 - t
        remote(qq.at[0], qq.at[mask], qs.at[mask], qr.at[mask], to_c).wait_recv()
        weighted, centred, stats = attend(mask)
        send[mask, :, 0:hd] = weighted.astype(jnp.bfloat16)
        send[mask, :, hd:] = centred.astype(jnp.bfloat16)
        sstat[mask] = stats
        for copy in result_copies(mask):
            copy.start()
        return carry

    lax.fori_loop(0, zc - 1, step, 0)
    own_w, own_c, own_stats = attend(0)
    recv[0, :, 0:hd] = own_w.astype(jnp.bfloat16)
    recv[0, :, hd:] = own_c.astype(jnp.bfloat16)
    rstat[0] = own_stats
    for m in range(1, zc):
        for copy in result_copies(m):
            copy.wait_recv()

    peaks = [rstat[m, 0:1, :] for m in range(zc)]
    peak = functools.reduce(jnp.maximum, peaks)
    shares = [jnp.exp2((pk - peak) * factor) for pk in peaks]
    total = sum(a * rstat[m, 1:2, :] for m, a in enumerate(shares))
    mean = sum(a * rstat[m, 1:2, :] * rstat[m, 2:3, :] for m, a in enumerate(shares)) / total
    coef[...] = jnp.zeros_like(coef)
    for m, a in enumerate(shares):
        a = a / total
        coef[2 * m : 2 * m + 1, :] = a
        coef[2 * m + 1 : 2 * m + 2, :] = a * (rstat[m, 2:3, :] - mean)
    columns = coef[...].T
    out = outt = 0.0
    for m in range(zc):
        w = recv[m, :, 0:hd].astype(jnp.float32)
        d = recv[m, :, hd:].astype(jnp.float32)
        a, g = columns[:, 2 * m : 2 * m + 1], columns[:, 2 * m + 1 : 2 * m + 2]
        out = out + a * w
        outt = outt + (a * d + g * w)
    out_ref[...] = out.astype(out_ref.dtype)
    outt_ref[...] = outt.astype(outt_ref.dtype)
    for copy in sent:
        copy.wait_send()
    bias_copy.wait_send()
    for m in range(1, zc):
        for copy in result_copies(m):
            copy.wait_send()


def shards(
    queries, query_tangent, keys, values, key_tangent, value_tangent, block_list, block_count
):
    rows, hd = keys.shape
    shard_blocks = rows // BLK
    slabs, pbs = lax.axis_size("kv"), lax.axis_size("pb")
    zc = slabs // 2
    slab_blocks = pbs * shard_blocks
    ids = block_list[:, 0, :]
    shard_id = ids // shard_blocks
    local = shard_id // slabs * shard_blocks + ids % shard_blocks
    used = jnp.arange(ids.shape[1])[None, :] < block_count
    on = jnp.any(
        (local[:, :, None] == jnp.arange(slab_blocks)[None, None, :]) & used[:, :, None], axis=1
    )
    on = on.reshape(zc, 2, shard_blocks, pbs, shard_blocks).transpose(1, 3, 0, 2, 4)
    on = on.reshape(2, pbs, zc, shard_blocks, shard_blocks, 1)
    bias = jnp.broadcast_to(
        jnp.where(on, 0.0, -1e30).astype(jnp.float32), on.shape[:-1] + (BLK,)
    ).reshape(2, pbs, zc, shard_blocks, rows)
    vmem = pl.BlockSpec(memory_space=pltpu.VMEM)
    hbm = pl.BlockSpec(memory_space=pl.ANY)
    dma = pltpu.SemaphoreType.DMA
    out = jax.ShapeDtypeStruct((rows, hd), jnp.bfloat16)
    return pl.pallas_call(
        functools.partial(kernel, zc),
        out_shape=(out, out),
        in_specs=[hbm] * 6 + [vmem],
        out_specs=(vmem, vmem),
        scratch_shapes=[
            pltpu.VMEM((8, rows, 4 * hd), jnp.bfloat16),
            pltpu.VMEM((zc, rows, 2 * hd), jnp.bfloat16),
            pltpu.VMEM((pbs, zc, shard_blocks, rows), jnp.float32),
            pltpu.VMEM((rows, 8 * rows), jnp.float32),
            pltpu.VMEM((rows, 8 * rows), jnp.bfloat16),
            pltpu.VMEM((rows, 8 * rows), jnp.bfloat16),
            pltpu.VMEM((zc, rows, 2 * hd), jnp.bfloat16),
            pltpu.VMEM((zc, 8, rows), jnp.float32),
            pltpu.VMEM((zc, rows, 2 * hd), jnp.bfloat16),
            pltpu.VMEM((zc, 8, rows), jnp.float32),
            pltpu.VMEM((128, rows), jnp.float32),
            dma((6,)),
            dma((8, 2)),
            dma((8, 2)),
            dma((zc,)),
            dma((zc,)),
            dma((2,)),
            dma((zc,)),
            dma((zc,)),
            dma((zc,)),
            dma((zc,)),
        ],
        compiler_params=pltpu.CompilerParams(
            collective_id=0, has_side_effects=True, vmem_limit_bytes=40 * 1024 * 1024
        ),
    )(queries, query_tangent, keys, values, key_tangent, value_tangent, bias)


def solution(mesh):
    rows = P(("pb", "kv"), None)
    return jax.shard_map(
        shards,
        mesh=mesh,
        in_specs=(rows,) * 6 + (P("pb", "kv", None), P("pb", "kv")),
        out_specs=(rows, rows),
        check_vma=False,
    )
```

```python
import functools
import math

import jax
import jax.numpy as jnp
from jax import lax
from jax.experimental import pallas as pl
from jax.experimental.pallas import tpu as pltpu
from jax.sharding import PartitionSpec as P

BLK = 128
NT = (((1,), (1,)), ((), ()))
MESH = pl.DeviceIdType.MESH


def flip(a, b, bits):
    out = 0
    for k in range(bits):
        w = 1 << k
        out = out + (a // w + b // w) % 2 * w
    return out


def kernel(
    zc, slabs, q_in, qt_in, k_in, v_in, kt_in, vt_in, list_in, count_in, out_ref,
    kv, qq, lst, cnt, bias, s_scr, p_scr, ps_scr, send, sstat, recv, rstat, coef,
    local_sem, ks, kr, qs, qr, bs, rs, rr, ts, tr,
):
    rows, hd = q_in.shape
    half = rows // 2
    bits = zc.bit_length() - 1
    scale = 1.0 / math.sqrt(hd)
    factor = scale * math.log2(math.e)
    pb, kvi = lax.axis_index("pb"), lax.axis_index("kv")
    y, c, z, x = pb // 2, pb % 2, kvi // 2, kvi % 2
    to_x = (pb, kvi + 1 - 2 * x)
    to_y = (pb + 2 - 4 * y, kvi)
    to_c = (pb + 1 - 2 * c, kvi)

    def to_z(mask):
        return (pb, flip(z, mask, bits) * 2 + x)

    loads = []
    for n, (src, dst) in enumerate(
        [
            (k_in, kv.at[0, :, pl.ds(0, hd)]),
            (kt_in, kv.at[0, :, pl.ds(hd, hd)]),
            (v_in, kv.at[0, :, pl.ds(2 * hd, hd)]),
            (vt_in, kv.at[0, :, pl.ds(3 * hd, hd)]),
            (qt_in, qq.at[0, :, pl.ds(0, hd)]),
            (q_in, qq.at[0, :, pl.ds(hd, hd)]),
            (list_in, lst.at[0]),
            (count_in, cnt.at[0]),
        ]
    ):
        copy = pltpu.make_async_copy(src, dst, local_sem.at[n])
        copy.start()
        loads.append(copy)

    barrier = pltpu.get_barrier_semaphore()
    for dev in [to_x, to_y, to_c] + [to_z(m) for m in range(1, zc)]:
        pl.semaphore_signal(barrier, inc=1, device_id=dev, device_id_type=MESH)
    pl.semaphore_wait(barrier, 2 + zc)
    for copy in loads:
        copy.wait()

    def remote(src, dst, ssem, rsem, dev):
        return pltpu.make_async_remote_copy(
            src_ref=src, dst_ref=dst, send_sem=ssem, recv_sem=rsem,
            device_id=dev, device_id_type=MESH,
        )

    sent = []

    def piece(slot, h):
        return kv.at[slot, pl.ds(h * half, half)]

    def give(slot, h, dst, dev):
        copy = remote(piece(slot, h), piece(dst, h), ks.at[dst, h], kr.at[dst, h], dev)
        copy.start()
        sent.append(copy)

    def got(slot, h):
        remote(piece(slot, h), piece(slot, h), ks.at[slot, h], kr.at[slot, h], to_c).wait_recv()

    give(0, 1, 1, to_x)
    give(0, 0, 2, to_y)
    give(0, 0, 1, to_x)
    give(0, 1, 2, to_y)
    for m in range(zc - 1, 0, -1):
        copy = remote(qq.at[0], qq.at[m], qs.at[m], qr.at[m], to_z(m))
        copy.start()
        sent.append(copy)
    give(0, 0, 4, to_c)
    give(0, 1, 4, to_c)
    tables = [
        remote(lst.at[0], lst.at[1], bs.at[0], bs.at[1], to_x),
        remote(cnt.at[0], cnt.at[1], bs.at[2], bs.at[3], to_x),
    ]
    for copy in tables:
        copy.start()

    def mask_rows(side):
        blocks = lst.shape[2]
        shard_blocks = rows // BLK
        slab_blocks = 4 * shard_blocks
        ids = lst[side]
        local = ids // (shard_blocks * slabs) * shard_blocks + ids % shard_blocks
        used = lax.broadcasted_iota(jnp.int32, ids.shape, 0) < cnt[side]
        row = lax.broadcasted_iota(jnp.int32, (slab_blocks, blocks), 0)
        on = jnp.zeros((slab_blocks, blocks), jnp.float32)
        for g in range(slab_blocks):
            hit = jnp.max(jnp.where((local == g) & used, 1.0, 0.0), axis=0, keepdims=True)
            on = jnp.where(row == g, hit, on)
        spread = jnp.where(
            lax.broadcasted_iota(jnp.int32, (slab_blocks, 4 * rows), 1) // BLK
            == lax.broadcasted_iota(jnp.int32, (slab_blocks, 4 * rows), 0),
            1.0, 0.0,
        )
        full = lax.dot_general(
            on, spread, (((0,), (0,)), ((), ())), preferred_element_type=jnp.float32
        )
        full = (full - 1.0) * 1e30
        for g in range(blocks):
            for p in range(4):
                bias[side, g, p] = full[g : g + 1, p * rows : (p + 1) * rows]

    mask_rows(0)
    got(2, 0)
    give(2, 0, 3, to_x)
    give(2, 0, 6, to_c)
    got(1, 1)
    give(1, 1, 3, to_y)
    give(1, 1, 5, to_c)
    got(1, 0)
    give(1, 0, 5, to_c)
    got(2, 1)
    give(2, 1, 6, to_c)
    for copy in tables:
        copy.wait_recv()
    mask_rows(1)

    def partial(mask, slots):
        zt = flip(z, mask, bits)
        best = None
        for n, r in enumerate(slots):
            pbr = flip(pb, (r // 2) % 2 * 2 + r // 4, 2)
            s = lax.dot_general(
                qq[mask, :, hd:], kv[r, :, 0:hd], NT, preferred_element_type=jnp.float32
            )
            s = jnp.concatenate(
                [
                    s[h * half : (h + 1) * half] + bias[r % 2, (zt * 2 + x) * 2 + h, pbr]
                    for h in range(2)
                ],
                axis=0,
            )
            s_scr[:, n * rows : (n + 1) * rows] = s
            top = jnp.maximum(s[:, :hd], s[:, hd:])
            best = top if best is None else jnp.maximum(best, top)
        peak = jnp.max(best, axis=1, keepdims=True)
        total = slope = None
        for n, r in enumerate(slots):
            p = jnp.exp2((s_scr[:, n * rows : (n + 1) * rows] - peak) * factor)
            t = lax.dot_general(
                qq[mask], kv[r, :, 0 : 2 * hd], NT, preferred_element_type=jnp.float32
            )
            pt = p * t
            p_scr[:, n * rows : (n + 1) * rows] = p.astype(jnp.bfloat16)
            ps_scr[:, n * rows : (n + 1) * rows] = pt.astype(jnp.bfloat16)
            p2 = p[:, :hd] + p[:, hd:]
            pt2 = pt[:, :hd] + pt[:, hd:]
            total = p2 if total is None else total + p2
            slope = pt2 if slope is None else slope + pt2
        total = jnp.sum(total, axis=1, keepdims=True)
        slope = jnp.sum(slope, axis=1, keepdims=True)
        lo, size = slots[0], len(slots)
        both = jnp.dot(
            p_scr[:, 0 : size * rows],
            kv[lo : lo + size, :, 2 * hd :].reshape(size * rows, 2 * hd),
            preferred_element_type=jnp.float32,
        )
        tang = jnp.dot(
            ps_scr[:, 0 : size * rows],
            kv[lo : lo + size, :, 2 * hd : 3 * hd].reshape(size * rows, hd),
            preferred_element_type=jnp.float32,
        )
        return peak, total, slope, both[:, :hd], tang * scale + both[:, hd:]

    def close(peak, total, slope, weighted, tang):
        mean = slope * scale / total
        centred = tang - mean * weighted
        lane = lax.broadcasted_iota(jnp.int32, (rows, hd), 1)
        stats = jnp.where(lane == 0, peak, jnp.where(lane == 1, total, mean))
        return weighted, centred, stats.T[0:8]

    def attend(mask):
        return close(*partial(mask, range(8)))

    def join(a, b):
        peak = jnp.maximum(a[0], b[0])
        fa, fb = jnp.exp2((a[0] - peak) * factor), jnp.exp2((b[0] - peak) * factor)
        return (peak,) + tuple(fa * m + fb * n for m, n in zip(a[1:], b[1:]))

    def result_copies(mask):
        dev = to_z(mask)
        return (
            remote(send.at[mask], recv.at[mask], rs.at[mask], rr.at[mask], dev),
            remote(sstat.at[mask], rstat.at[mask], ts.at[mask], tr.at[mask], dev),
        )

    def hand_in(mask, weighted, centred, stats):
        send[mask, :, 0:hd] = weighted.astype(jnp.bfloat16)
        send[mask, :, hd:] = centred.astype(jnp.bfloat16)
        sstat[mask] = stats
        for copy in result_copies(mask):
            copy.start()

    def got_queries(mask):
        remote(qq.at[0], qq.at[mask], qs.at[mask], qr.at[mask], to_c).wait_recv()

    far = zc - 1
    got_queries(far)
    for slot in (4, 5, 6):
        for h in range(2):
            got(slot, h)
    early = join(partial(far, (0, 1, 2)), partial(far, (4, 5, 6)))
    for h in range(2):
        got(3, h)
        give(3, h, 7, to_c)
    early = join(early, partial(far, (3,)))
    for h in range(2):
        got(7, h)
    hand_in(far, *close(*join(early, partial(far, (7,)))))

    def step(t, carry):
        mask = zc - 1 - t
        got_queries(mask)
        hand_in(mask, *attend(mask))
        return carry

    lax.fori_loop(1, zc - 1, step, 0)
    own_w, own_c, own_stats = attend(0)
    recv[0, :, 0:hd] = own_w.astype(jnp.bfloat16)
    recv[0, :, hd:] = own_c.astype(jnp.bfloat16)
    rstat[0] = own_stats
    for m in range(1, zc):
        for copy in result_copies(m):
            copy.wait_recv()

    peaks = [rstat[m, 0:1, :] for m in range(zc)]
    peak = functools.reduce(jnp.maximum, peaks)
    shares = [jnp.exp2((pk - peak) * factor) for pk in peaks]
    total = sum(a * rstat[m, 1:2, :] for m, a in enumerate(shares))
    mean = sum(a * rstat[m, 1:2, :] * rstat[m, 2:3, :] for m, a in enumerate(shares)) / total
    coef[...] = jnp.zeros_like(coef)
    for m, a in enumerate(shares):
        a = a / total
        coef[2 * m : 2 * m + 1, :] = a
        coef[2 * m + 1 : 2 * m + 2, :] = a * (rstat[m, 2:3, :] - mean)
    columns = coef[...].T
    out = outt = 0.0
    for m in range(zc):
        w = recv[m, :, 0:hd].astype(jnp.float32)
        d = recv[m, :, hd:].astype(jnp.float32)
        a, g = columns[:, 2 * m : 2 * m + 1], columns[:, 2 * m + 1 : 2 * m + 2]
        out = out + a * w
        outt = outt + (a * d + g * w)
    out_ref[:, 0:hd] = out.astype(out_ref.dtype)
    out_ref[:, hd:] = outt.astype(out_ref.dtype)
    for copy in sent:
        copy.wait_send()
    for copy in tables:
        copy.wait_send()
    for m in range(1, zc):
        for copy in result_copies(m):
            copy.wait_send()


def shards(
    queries, query_tangent, keys, values, key_tangent, value_tangent, block_list, block_count
):
    rows, hd = keys.shape
    slabs, pbs = lax.axis_size("kv"), lax.axis_size("pb")
    zc = slabs // 2
    list_t = block_list[:, 0, :].T
    count_t = block_count.T
    blocks = list_t.shape[1]
    vmem = pl.BlockSpec(memory_space=pltpu.VMEM)
    hbm = pl.BlockSpec(memory_space=pl.ANY)
    dma = pltpu.SemaphoreType.DMA
    out = pl.pallas_call(
        functools.partial(kernel, zc, slabs),
        out_shape=jax.ShapeDtypeStruct((rows, 2 * hd), jnp.bfloat16),
        in_specs=[hbm] * 8,
        out_specs=vmem,
        scratch_shapes=[
            pltpu.VMEM((8, rows, 4 * hd), jnp.bfloat16),
            pltpu.VMEM((zc, rows, 2 * hd), jnp.bfloat16),
            pltpu.VMEM((2,) + list_t.shape, jnp.int32),
            pltpu.VMEM((2, 1, blocks), jnp.int32),
            pltpu.VMEM((2, blocks, pbs, 1, rows), jnp.float32),
            pltpu.VMEM((rows, 8 * rows), jnp.float32),
            pltpu.VMEM((rows, 8 * rows), jnp.bfloat16),
            pltpu.VMEM((rows, 8 * rows), jnp.bfloat16),
            pltpu.VMEM((zc, rows, 2 * hd), jnp.bfloat16),
            pltpu.VMEM((zc, 8, rows), jnp.float32),
            pltpu.VMEM((zc, rows, 2 * hd), jnp.bfloat16),
            pltpu.VMEM((zc, 8, rows), jnp.float32),
            pltpu.VMEM((128, rows), jnp.float32),
            dma((8,)),
            dma((8, 2)),
            dma((8, 2)),
            dma((zc,)),
            dma((zc,)),
            dma((4,)),
            dma((zc,)),
            dma((zc,)),
            dma((zc,)),
            dma((zc,)),
        ],
        compiler_params=pltpu.CompilerParams(
            collective_id=0, has_side_effects=True, vmem_limit_bytes=62 * 1024 * 1024
        ),
    )(queries, query_tangent, keys, values, key_tangent, value_tangent, list_t, count_t)
    return out[:, :hd], out[:, hd:]


def solution(mesh):
    rows = P(("pb", "kv"), None)
    return jax.shard_map(
        shards,
        mesh=mesh,
        in_specs=(rows,) * 6 + (P("pb", "kv", None), P("pb", "kv")),
        out_specs=(rows, rows),
        check_vma=False,
    )
```
